32 devices in a mesh: grp: 4 (over y, x), gx: 4 (over z), gy: 2 (over core).
Axes of the slice: x: 2, y: 2, z: 4, core: 2. Of those that a mesh axis runs over, the one named last changes fastest.
Arguments:
- coarse_modes: float32 [4, 2, 8, 32, 4096], P('grp', None, None, 'gy', 'gx'), may hold values from -6 to 6
- salinity: float32 [32, 128, 16384], P('grp', 'gy', 'gx'), may hold values from -6 to 6
- viscosity: float32 [4], P('grp'), may hold values from 0.1 to 1
- forcing_gain: float32 [4], P('grp'), may hold values from 0.5 to 2
- diffusivity: float32 [32], P('grp'), may hold values from 0.3 to 1.5
Outputs:
- salinity_next: float32 [32, 128, 16384], P('grp', 'gy', 'gx')
- coarse_next: float32 [4, 2, 8, 32, 4096], P('grp', None, None, 'gy', 'gx')
The draws below stay inside these ranges and needn't reach their ends.
All inputs are finite; a program needn't handle non-finite values.
Results may differ from the reference program's by a relative error of at most 0.0003.
Values sent between devices are 32-bit elements; how exact they have to be, the bound alone decides.
A program may use at most 192 MiB of HBM per device.

```python
import math
import jax
import jax.numpy as jnp
from jax import lax

FIELDS = 4
NV = 4096
RATIO = 4
LV = 8
NYC = 32
NZF = 32
NYF = 128
NXF = 16384


def shard_levels(own_key, dims, split, low, high):
    def one(dim, parts):
        draws = jax.random.uniform(jax.random.fold_in(jax.random.fold_in(own_key, 6), dim), (parts,), jnp.float32, low / len(split), high / len(split))
        return jnp.repeat(jnp.exp(draws), dims[dim] // parts).reshape((-1,) + (1,) * (len(dims) - dim - 1))

    gain = one(*split[0])
    for cut in split[1:]:
        gain = gain * one(*cut)
    return gain


def noise(stream_key, shape, scale, reach, shards=(), kind=jnp.bfloat16):
    entries = jax.random.normal(stream_key, shape, jnp.float32) * scale
    if len(shards) > 0:
        entries = shard_levels(stream_key, shape, shards, -0.22, 0.18) * entries
    return jnp.clip(entries, min=-reach, max=reach).astype(kind)


def setup_inputs(seed: int = 0) -> dict:
    splits = jax.random.split(jax.random.key(seed), 6)
    return {
        "coarse_modes": noise(splits[0], (FIELDS, 2, LV, NYC, NV), 1.0, 6.0, ((0, 4), (3, 2), (4, 4)), jnp.float32),
        "salinity": noise(splits[1], (NZF, NYF, NXF), 1.0, 6.0, ((0, 4), (1, 2), (2, 4)), jnp.float32),
        "viscosity": jnp.clip(jnp.exp(math.log(1.0) - 2.3025851 * jax.random.uniform(splits[2], (FIELDS,), jnp.float32) ** shard_levels(splits[2], (FIELDS,), ((0, 4),), -0.2, 0.2)), 0.1, 1.0),
        "forcing_gain": jnp.clip(0.5 + 1.5 * jax.random.uniform(splits[3], (FIELDS,), jnp.float32) ** shard_levels(splits[3], (FIELDS,), ((0, 4),), -0.2, 0.2), 0.5, 2.0),
        "diffusivity": jnp.clip(jnp.exp(math.log(1.5) - 1.60943787 * jax.random.uniform(splits[4], (NZF,), jnp.float32) ** shard_levels(splits[4], (NZF,), ((0, 4),), -0.2, 0.2)), 0.3, 1.5),
    }


fine_step = 0.1


def refine(coarse, dimension):
    extent = coarse.shape[dimension]
    pieces = []
    for sub_cell in range(RATIO):
        offset = (sub_cell + 0.5) / RATIO - 0.5
        beside = jnp.roll(coarse, -1 if offset > 0 else 1, axis=dimension)
        pieces.append((1.0 - abs(offset)) * coarse + abs(offset) * beside)
    stacked = jnp.stack(pieces, axis=dimension + 1)
    target = list(coarse.shape)
    target[dimension] = extent * RATIO
    return stacked.reshape(target)


def reference(coarse_modes, salinity, viscosity, forcing_gain, diffusivity):
    spectral = lax.complex(coarse_modes[:, 0], coarse_modes[:, 1])
    physical = jnp.real(jnp.fft.ifft(spectral, axis=-1, norm="ortho"))

    def update(fine_level):
        coarse_plane = lax.dynamic_index_in_dim(physical, fine_level // RATIO, 1, keepdims=False)
        velocity = refine(refine(coarse_plane, 1), 2)
        centre = lax.dynamic_index_in_dim(salinity, fine_level, 0, keepdims=False)
        upper_cells = lax.dynamic_index_in_dim(salinity, (fine_level + 1) % NZF, 0, keepdims=False)
        lower_cells = lax.dynamic_index_in_dim(salinity, (fine_level + NZF - 1) % NZF, 0, keepdims=False)
        east_cells = jnp.roll(centre, -1, axis=1)
        west_cells = jnp.roll(centre, 1, axis=1)
        north_cells = jnp.roll(centre, -1, axis=0)
        south_cells = jnp.roll(centre, 1, axis=0)
        diffuse_rate = lax.dynamic_index_in_dim(diffusivity, fine_level, 0, keepdims=False)
        spread = diffuse_rate * (east_cells + west_cells + north_cells + south_cells + upper_cells + lower_cells - 6.0 * centre)
        advection = velocity[0] * (east_cells - west_cells) * 0.5 + velocity[1] * (north_cells - south_cells) * 0.5 + velocity[2] * (upper_cells - lower_cells) * 0.5
        updated = centre + fine_step * (spread - advection)
        buoyancy = velocity[3] - updated
        restricted = buoyancy.reshape(NYC, RATIO, NV, RATIO).mean(axis=(1, 3))
        return updated, restricted

    salinity_next, restricted = lax.map(update, jnp.arange(NZF, dtype=jnp.int32))
    buoyancy = restricted.reshape(LV, RATIO, NYC, NV).mean(axis=1)
    spectrum = jnp.fft.fft(buoyancy, axis=-1, norm="ortho")
    spectral_parts = jnp.stack([jnp.real(spectrum), jnp.imag(spectrum)])
    mode_index = jnp.arange(NV, dtype=jnp.int32)
    wavenumber = jnp.where(mode_index < NV // 2, mode_index, mode_index - NV)
    scaled_wave = (2.0 * math.pi / NV) * wavenumber.astype(jnp.float32)
    damping = jnp.exp(-viscosity[:, None] * scaled_wave[None, :] * scaled_wave[None, :])
    coarse_next = damping[:, None, None, None, :] * coarse_modes + forcing_gain[:, None, None, None, None] * spectral_parts[None]
    return salinity_next, coarse_next
```

```python
import math

import jax
import jax.numpy as jnp
from jax import lax
from jax.experimental import pallas as pl
from jax.experimental.pallas import tpu as pltpu
from jax.sharding import PartitionSpec as P

RATIO = 4


fine_step = 0.1


def extended(cells, sides, width):
    for axis, dim in sides:
        count = lax.axis_size(axis)
        head = lax.slice_in_dim(cells, 0, width, axis=dim)
        tail = lax.slice_in_dim(cells, cells.shape[dim] - width, cells.shape[dim], axis=dim)
        cells = jnp.concatenate(
            [
                lax.ppermute(tail, axis, [(i, (i + 1) % count) for i in range(count)]),
                cells,
                lax.ppermute(head, axis, [((i + 1) % count, i) for i in range(count)]),
            ],
            axis=dim,
        )
    return cells


def circle_table(row_count, col_count, period, orient):
    product = (
        lax.broadcasted_iota(jnp.int32, (row_count, col_count), 0)
        * lax.broadcasted_iota(jnp.int32, (row_count, col_count), 1)
        % period
    )
    angle = 2.0 * math.pi / period * product.astype(jnp.float32)
    return (jnp.cos(angle), orient * jnp.sin(angle))


def contract(data, table, form):
    return jnp.einsum(form, data, table, precision=lax.Precision.HIGH)


def fourier_lines(real_part, imag_part, orient, want_imag):
    length = real_part.shape[-1]
    exponent = length.bit_length() - 1
    inner_count = 2 ** ((exponent + 2) // 2)
    outer_count = length // inner_count
    leading = real_part.shape[:-1]
    cos_outer, sin_outer = circle_table(outer_count, outer_count, outer_count, orient)
    cos_twist, sin_twist = circle_table(outer_count, inner_count, length, orient)
    cos_inner, sin_inner = circle_table(inner_count, inner_count, inner_count, orient)
    first_form = "...ba,bk->...ka"
    second_form = "...ka,aj->...jk"
    split_real = real_part.reshape(leading + (outer_count, inner_count))
    section_real = contract(split_real, cos_outer, first_form)
    section_imag = contract(split_real, sin_outer, first_form)
    if imag_part is not None:
        split_imag = imag_part.reshape(leading + (outer_count, inner_count))
        section_real = section_real - contract(split_imag, sin_outer, first_form)
        section_imag = section_imag + contract(split_imag, cos_outer, first_form)
    twist_real = section_real * cos_twist - section_imag * sin_twist
    twist_imag = section_real * sin_twist + section_imag * cos_twist
    norm_factor = length ** (-0.5)
    final_real = (
        contract(twist_real, cos_inner, second_form) - contract(twist_imag, sin_inner, second_form)
    ) * norm_factor
    if not want_imag:
        return final_real.reshape(leading + (length,))
    final_imag = (
        contract(twist_real, sin_inner, second_form) + contract(twist_imag, cos_inner, second_form)
    ) * norm_factor
    return (final_real.reshape(leading + (length,)), final_imag.reshape(leading + (length,)))


def spread_table(cell_count, source_count):
    fine_count = cell_count * RATIO
    source = lax.broadcasted_iota(jnp.int32, (source_count, fine_count), 0)
    fine_cell = lax.broadcasted_iota(jnp.int32, (source_count, fine_count), 1)
    parent = fine_cell // RATIO
    sub_cell = (fine_cell % RATIO).astype(jnp.float32)
    offset = (sub_cell + 0.5) / RATIO - 0.5
    magnitude = jnp.abs(offset)
    own_weight = jnp.where(source == parent + 1, 1.0 - magnitude, 0.0)
    after_weight = jnp.where((source == parent + 2) & (offset > 0), magnitude, 0.0)
    before_weight = jnp.where((source == parent) & (offset < 0), magnitude, 0.0)
    return (own_weight + after_weight + before_weight).astype(jnp.bfloat16)


def average_table(fine_count, weight):
    fine_cell = lax.broadcasted_iota(jnp.int32, (fine_count, fine_count // RATIO), 0)
    coarse_cell = lax.broadcasted_iota(jnp.int32, (fine_count, fine_count // RATIO), 1)
    return jnp.where(fine_cell // RATIO == coarse_cell, weight, 0.0).astype(jnp.bfloat16)


def split_parts(value):
    high = value.astype(jnp.bfloat16)
    return high, (value - high.astype(jnp.float32)).astype(jnp.bfloat16)


def product(left, right):
    return jnp.dot(left, right, preferred_element_type=jnp.float32)


def step_kernel(
    cells_coarse,
    diff_ref,
    centre_ref,
    below_ref,
    above_ref,
    lower_ref,
    upper_ref,
    south_ref,
    north_ref,
    west_ref,
    east_ref,
    rim_ref,
    ty_ref,
    tx_ref,
    ry_ref,
    rx_ref,
    out_ref,
    coarse_ref,
    vel_ref,
    acc_ref,
):
    level = pl.program_id(0)
    last = pl.num_programs(0) - 1
    part = lax.rem(level, RATIO)
    rows, cols = centre_ref.shape[1], centre_ref.shape[2]
    fine = cells_coarse * RATIO
    chunks = cols // fine
    span = tx_ref.shape[0]

    @pl.when(part == 0)
    def _():
        for field in range(rim_ref.shape[0]):
            high, low = split_parts(rim_ref[field, 0])
            along = product(ty_ref[...], high) + product(ty_ref[...], low)
            high, low = split_parts(along)
            for k in range(chunks):
                window = slice(k * cells_coarse, k * cells_coarse + span)
                vel_ref[field, :, k * fine : (k + 1) * fine] = product(
                    high[:, window], tx_ref[...]
                ) + product(low[:, window], tx_ref[...])
        acc_ref[...] = jnp.zeros_like(acc_ref)

    rate = diff_ref[level]
    row_at = lax.broadcasted_iota(jnp.int32, (rows, fine), 0)
    lane_at = lax.broadcasted_iota(jnp.int32, (rows, fine), 1)
    first_lane, last_lane = lane_at == 0, lane_at == fine - 1
    first_row, last_row = row_at == 0, row_at == rows - 1
    bottom, top = level == 0, level == last
    for k in range(chunks):
        start, stop = k * fine, (k + 1) * fine
        centre = centre_ref[0, :, start:stop]
        before = west_ref[0] if k == 0 else centre_ref[0, :, start - 1 : start]
        after = east_ref[0] if k == chunks - 1 else centre_ref[0, :, stop : stop + 1]
        west = jnp.where(first_lane, before, pltpu.roll(centre, 1, 1))
        east = jnp.where(last_lane, after, pltpu.roll(centre, fine - 1, 1))
        south = jnp.where(first_row, south_ref[0, :, start:stop], pltpu.roll(centre, 1, 0))
        north = jnp.where(
            last_row, north_ref[0, :, start:stop], pltpu.roll(centre, rows - 1, 0)
        )
        lower = jnp.where(bottom, lower_ref[0, :, start:stop], below_ref[0, :, start:stop])
        upper = jnp.where(top, upper_ref[0, :, start:stop], above_ref[0, :, start:stop])
        spread = rate * (east + west + north + south + upper + lower - 6.0 * centre)
        advection = (
            vel_ref[0, :, start:stop] * (east - west)
            + vel_ref[1, :, start:stop] * (north - south)
            + vel_ref[2, :, start:stop] * (upper - lower)
        ) * 0.5
        updated = centre + fine_step * (spread - advection)
        out_ref[0, :, start:stop] = updated
        acc_ref[:, start:stop] += vel_ref[3, :, start:stop] - updated

    @pl.when(part == RATIO - 1)
    def _():
        for k in range(chunks):
            high, low = split_parts(acc_ref[:, k * fine : (k + 1) * fine])
            half = product(ry_ref[...], high) + product(ry_ref[...], low)
            high, low = split_parts(half)
            coarse_ref[0, :, k * cells_coarse : (k + 1) * cells_coarse] = product(
                high, rx_ref[...]
            ) + product(low, rx_ref[...])


def fine_update(rimmed, salinity, halos, diffusivity):
    levels, rows, cols = salinity.shape
    fields, quarter, rim_rows, rim_cols = rimmed.shape
    row_count, width = rim_rows - 2, rim_cols - 2
    cells_coarse = min(128, width)
    fine = cells_coarse * RATIO
    span = cells_coarse + 128
    row_pad = -rim_rows % 16
    rimmed = jnp.pad(rimmed, ((0, 0), (0, 0), (0, row_pad), (0, width + 128 - rim_cols)))
    ty = spread_table(row_count, rim_rows + row_pad).T
    tx = spread_table(cells_coarse, span)
    ry = average_table(rows, 1.0 / RATIO).T
    rx = average_table(fine, 1.0 / RATIO / RATIO)

    def fixed(array):
        return pl.BlockSpec(array.shape, lambda i: (0,) * array.ndim)

    def level_block(array):
        return pl.BlockSpec((1,) + array.shape[1:], lambda i: (i, 0, 0))

    slab = (1, rows, cols)
    lower, upper, south, north, west, east = halos
    return pl.pallas_call(
        lambda *refs: step_kernel(cells_coarse, *refs),
        grid=(levels,),
        in_specs=[
            pl.BlockSpec(memory_space=pltpu.SMEM),
            pl.BlockSpec(slab, lambda i: (i, 0, 0)),
            pl.BlockSpec(slab, lambda i: (jnp.maximum(i - 1, 0), 0, 0)),
            pl.BlockSpec(slab, lambda i: (jnp.minimum(i + 1, levels - 1), 0, 0)),
            fixed(lower),
            fixed(upper),
            level_block(south),
            level_block(north),
            level_block(west),
            level_block(east),
            pl.BlockSpec((fields, 1) + rimmed.shape[2:], lambda i: (0, i // RATIO, 0, 0)),
            fixed(ty),
            fixed(tx),
            fixed(ry),
            fixed(rx),
        ],
        out_specs=[
            pl.BlockSpec(slab, lambda i: (i, 0, 0)),
            pl.BlockSpec((1, row_count, width), lambda i: (i // RATIO, 0, 0)),
        ],
        out_shape=[
            jax.ShapeDtypeStruct(salinity.shape, jnp.float32),
            jax.ShapeDtypeStruct((quarter, row_count, width), jnp.float32),
        ],
        scratch_shapes=[
            pltpu.VMEM((fields, rows, cols), jnp.float32),
            pltpu.VMEM((rows, cols), jnp.float32),
        ],
        compiler_params=pltpu.CompilerParams(
            dimension_semantics=("arbitrary",), vmem_limit_bytes=48 * 2**20
        ),
    )(
        diffusivity,
        salinity,
        salinity,
        salinity,
        lower,
        upper,
        south,
        north,
        west,
        east,
        rimmed,
        ty,
        tx,
        ry,
        rx,
    )


def side_layers(cells, axis, dim):
    count = lax.axis_size(axis)
    extent = cells.shape[dim]
    head = lax.slice_in_dim(cells, 0, 1, axis=dim)
    tail = lax.slice_in_dim(cells, extent - 1, extent, axis=dim)
    return (
        lax.ppermute(tail, axis, [(i, (i + 1) % count) for i in range(count)]),
        lax.ppermute(head, axis, [((i + 1) % count, i) for i in range(count)]),
    )


def per_device(coarse_modes, salinity, viscosity, forcing_gain, diffusivity):
    planes = coarse_modes.shape[2]
    row_count = coarse_modes.shape[3]
    width = coarse_modes.shape[4]
    groups = lax.axis_size("grp")
    quarter = planes // groups
    halos = (
        side_layers(salinity, "grp", 0)
        + side_layers(salinity, "gy", 1)
        + side_layers(salinity, "gx", 2)
    )
    pencil = lax.all_to_all(coarse_modes[0], "gx", split_axis=2, concat_axis=3, tiled=True)
    physical = fourier_lines(pencil[0], pencil[1], 1.0, False)
    blocks = lax.all_to_all(physical, "gx", split_axis=2, concat_axis=1, tiled=True)
    received = lax.all_to_all(
        blocks.reshape(groups, quarter, row_count, width),
        "grp",
        split_axis=0,
        concat_axis=0,
        tiled=True,
    )
    rimmed = extended(received, (("gx", 3), ("gy", 2)), 1)
    salinity_next, restricted = fine_update(rimmed, salinity, halos, diffusivity)
    columns = lax.all_to_all(restricted, "gx", split_axis=1, concat_axis=2, tiled=True)
    spec_real, spec_imag = fourier_lines(columns, None, -1.0, True)
    own_spectra = lax.all_to_all(
        jnp.stack([spec_real, spec_imag]), "gx", split_axis=3, concat_axis=2, tiled=True
    )
    spectrum = lax.all_gather(own_spectra, "grp", axis=1, tiled=True)
    total_modes = width * lax.axis_size("gx")
    mode_index = lax.axis_index("gx") * width + lax.broadcasted_iota(jnp.int32, (width,), 0)
    wavenumber = jnp.where(mode_index < total_modes // 2, mode_index, mode_index - total_modes)
    scaled_wave = 2.0 * math.pi / total_modes * wavenumber.astype(jnp.float32)
    damping = jnp.exp(-viscosity[0] * scaled_wave * scaled_wave)
    coarse_next = damping * coarse_modes + forcing_gain[0] * spectrum[None]
    return (salinity_next, coarse_next)


def solution(mesh):
    return jax.shard_map(
        per_device,
        mesh=mesh,
        in_specs=(
            P("grp", None, None, "gy", "gx"),
            P("grp", "gy", "gx"),
            P("grp"),
            P("grp"),
            P("grp"),
        ),
        out_specs=(P("grp", "gy", "gx"), P("grp", None, None, "gy", "gx")),
        check_vma=False,
    )
```

```python
import math

import jax
import jax.numpy as jnp
from jax import lax
from jax.experimental import pallas as pl
from jax.experimental.pallas import tpu as pltpu
from jax.sharding import PartitionSpec as P

RATIO = 4


fine_step = 0.1


def extended(cells, sides, width):
    for axis, dim in sides:
        count = lax.axis_size(axis)
        head = lax.slice_in_dim(cells, 0, width, axis=dim)
        tail = lax.slice_in_dim(cells, cells.shape[dim] - width, cells.shape[dim], axis=dim)
        cells = jnp.concatenate(
            [
                lax.ppermute(tail, axis, [(i, (i + 1) % count) for i in range(count)]),
                cells,
                lax.ppermute(head, axis, [((i + 1) % count, i) for i in range(count)]),
            ],
            axis=dim,
        )
    return cells


def circle_table(row_count, col_count, period, orient):
    product = (
        lax.broadcasted_iota(jnp.int32, (row_count, col_count), 0)
        * lax.broadcasted_iota(jnp.int32, (row_count, col_count), 1)
        % period
    )
    angle = 2.0 * math.pi / period * product.astype(jnp.float32)
    return (jnp.cos(angle), orient * jnp.sin(angle))


def contract(data, table, form):
    return jnp.einsum(form, data, table, precision=lax.Precision.HIGH)


def fourier_lines(real_part, imag_part, orient, want_imag):
    length = real_part.shape[-1]
    exponent = length.bit_length() - 1
    inner_count = 2 ** ((exponent + 2) // 2)
    outer_count = length // inner_count
    leading = real_part.shape[:-1]
    cos_outer, sin_outer = circle_table(outer_count, outer_count, outer_count, orient)
    cos_twist, sin_twist = circle_table(outer_count, inner_count, length, orient)
    cos_inner, sin_inner = circle_table(inner_count, inner_count, inner_count, orient)
    first_form = "...ba,bk->...ka"
    second_form = "...ka,aj->...jk"
    split_real = real_part.reshape(leading + (outer_count, inner_count))
    section_real = contract(split_real, cos_outer, first_form)
    section_imag = contract(split_real, sin_outer, first_form)
    if imag_part is not None:
        split_imag = imag_part.reshape(leading + (outer_count, inner_count))
        section_real = section_real - contract(split_imag, sin_outer, first_form)
        section_imag = section_imag + contract(split_imag, cos_outer, first_form)
    twist_real = section_real * cos_twist - section_imag * sin_twist
    twist_imag = section_real * sin_twist + section_imag * cos_twist
    norm_factor = length ** (-0.5)
    final_real = (
        contract(twist_real, cos_inner, second_form) - contract(twist_imag, sin_inner, second_form)
    ) * norm_factor
    if not want_imag:
        return final_real.reshape(leading + (length,))
    final_imag = (
        contract(twist_real, sin_inner, second_form) + contract(twist_imag, cos_inner, second_form)
    ) * norm_factor
    return (final_real.reshape(leading + (length,)), final_imag.reshape(leading + (length,)))


def spread_table(cell_count, source_count):
    fine_count = cell_count * RATIO
    source = lax.broadcasted_iota(jnp.int32, (source_count, fine_count), 0)
    fine_cell = lax.broadcasted_iota(jnp.int32, (source_count, fine_count), 1)
    parent = fine_cell // RATIO
    sub_cell = (fine_cell % RATIO).astype(jnp.float32)
    offset = (sub_cell + 0.5) / RATIO - 0.5
    magnitude = jnp.abs(offset)
    own_weight = jnp.where(source == parent + 1, 1.0 - magnitude, 0.0)
    after_weight = jnp.where((source == parent + 2) & (offset > 0), magnitude, 0.0)
    before_weight = jnp.where((source == parent) & (offset < 0), magnitude, 0.0)
    return (own_weight + after_weight + before_weight).astype(jnp.bfloat16)


def average_table(fine_count, weight):
    fine_cell = lax.broadcasted_iota(jnp.int32, (fine_count, fine_count // RATIO), 0)
    coarse_cell = lax.broadcasted_iota(jnp.int32, (fine_count, fine_count // RATIO), 1)
    return jnp.where(fine_cell // RATIO == coarse_cell, weight, 0.0).astype(jnp.bfloat16)


def split_parts(value):
    high = value.astype(jnp.bfloat16)
    return high, (value - high.astype(jnp.float32)).astype(jnp.bfloat16)


def product(left, right):
    return jnp.dot(left, right, preferred_element_type=jnp.float32)


def step_kernel(
    cells_coarse,
    diff_ref,
    centre_ref,
    below_ref,
    above_ref,
    lower_ref,
    upper_ref,
    south_ref,
    north_ref,
    west_ref,
    east_ref,
    rim_ref,
    ty_ref,
    tx_ref,
    ry_ref,
    rx_ref,
    out_ref,
    coarse_ref,
    vel_ref,
    acc_ref,
):
    level = pl.program_id(0)
    last = pl.num_programs(0) - 1
    part = lax.rem(level, RATIO)
    rows, cols = centre_ref.shape[1], centre_ref.shape[2]
    fine = cells_coarse * RATIO
    chunks = cols // fine
    span = tx_ref.shape[0]

    @pl.when(part == 0)
    def _():
        for field in range(rim_ref.shape[0]):
            high, low = split_parts(rim_ref[field, 0])
            along = product(ty_ref[...], high) + product(ty_ref[...], low)
            high, low = split_parts(along)
            for k in range(chunks):
                window = slice(k * cells_coarse, k * cells_coarse + span)
                vel_ref[field, :, k * fine : (k + 1) * fine] = product(
                    high[:, window], tx_ref[...]
                ) + product(low[:, window], tx_ref[...])
        acc_ref[...] = jnp.zeros_like(acc_ref)

    rate = diff_ref[level]
    row_at = lax.broadcasted_iota(jnp.int32, (rows, fine), 0)
    lane_at = lax.broadcasted_iota(jnp.int32, (rows, fine), 1)
    first_lane, last_lane = lane_at == 0, lane_at == fine - 1
    first_row, last_row = row_at == 0, row_at == rows - 1
    bottom, top = level == 0, level == last
    for k in range(chunks):
        start, stop = k * fine, (k + 1) * fine
        centre = centre_ref[0, :, start:stop]
        before = west_ref[0] if k == 0 else centre_ref[0, :, start - 1 : start]
        after = east_ref[0] if k == chunks - 1 else centre_ref[0, :, stop : stop + 1]
        west = jnp.where(first_lane, before, pltpu.roll(centre, 1, 1))
        east = jnp.where(last_lane, after, pltpu.roll(centre, fine - 1, 1))
        south = jnp.where(first_row, south_ref[0, :, start:stop], pltpu.roll(centre, 1, 0))
        north = jnp.where(
            last_row, north_ref[0, :, start:stop], pltpu.roll(centre, rows - 1, 0)
        )
        lower = jnp.where(bottom, lower_ref[0, :, start:stop], below_ref[0, :, start:stop])
        upper = jnp.where(top, upper_ref[0, :, start:stop], above_ref[0, :, start:stop])
        spread = rate * (east + west + north + south + upper + lower - 6.0 * centre)
        advection = (
            vel_ref[0, :, start:stop] * (east - west)
            + vel_ref[1, :, start:stop] * (north - south)
            + vel_ref[2, :, start:stop] * (upper - lower)
        ) * 0.5
        updated = centre + fine_step * (spread - advection)
        out_ref[0, :, start:stop] = updated
        acc_ref[:, start:stop] += vel_ref[3, :, start:stop] - updated

    @pl.when(part == RATIO - 1)
    def _():
        for k in range(chunks):
            high, low = split_parts(acc_ref[:, k * fine : (k + 1) * fine])
            half = product(ry_ref[...], high) + product(ry_ref[...], low)
            high, low = split_parts(half)
            coarse_ref[0, :, k * cells_coarse : (k + 1) * cells_coarse] = product(
                high, rx_ref[...]
            ) + product(low, rx_ref[...])


def fine_update(rimmed, salinity, halos, diffusivity):
    levels, rows, cols = salinity.shape
    fields, quarter, rim_rows, rim_cols = rimmed.shape
    row_count, width = rim_rows - 2, rim_cols - 2
    cells_coarse = min(128, width)
    fine = cells_coarse * RATIO
    span = cells_coarse + 128
    row_pad = -rim_rows % 16
    rimmed = jnp.pad(rimmed, ((0, 0), (0, 0), (0, row_pad), (0, width + 128 - rim_cols)))
    ty = spread_table(row_count, rim_rows + row_pad).T
    tx = spread_table(cells_coarse, span)
    ry = average_table(rows, 1.0 / RATIO).T
    rx = average_table(fine, 1.0 / RATIO / RATIO)

    def fixed(array):
        return pl.BlockSpec(array.shape, lambda i: (0,) * array.ndim)

    def level_block(array):
        return pl.BlockSpec((1,) + array.shape[1:], lambda i: (i, 0, 0))

    slab = (1, rows, cols)
    lower, upper, south, north, west, east = halos
    return pl.pallas_call(
        lambda *refs: step_kernel(cells_coarse, *refs),
        grid=(levels,),
        in_specs=[
            pl.BlockSpec(memory_space=pltpu.SMEM),
            pl.BlockSpec(slab, lambda i: (i, 0, 0)),
            pl.BlockSpec(slab, lambda i: (jnp.maximum(i - 1, 0), 0, 0)),
            pl.BlockSpec(slab, lambda i: (jnp.minimum(i + 1, levels - 1), 0, 0)),
            fixed(lower),
            fixed(upper),
            level_block(south),
            level_block(north),
            level_block(west),
            level_block(east),
            pl.BlockSpec((fields, 1) + rimmed.shape[2:], lambda i: (0, i // RATIO, 0, 0)),
            fixed(ty),
            fixed(tx),
            fixed(ry),
            fixed(rx),
        ],
        out_specs=[
            pl.BlockSpec(slab, lambda i: (i, 0, 0)),
            pl.BlockSpec((1, row_count, width), lambda i: (i // RATIO, 0, 0)),
        ],
        out_shape=[
            jax.ShapeDtypeStruct(salinity.shape, jnp.float32),
            jax.ShapeDtypeStruct((quarter, row_count, width), jnp.float32),
        ],
        scratch_shapes=[
            pltpu.VMEM((fields, rows, cols), jnp.float32),
            pltpu.VMEM((rows, cols), jnp.float32),
        ],
        compiler_params=pltpu.CompilerParams(
            dimension_semantics=("arbitrary",), vmem_limit_bytes=48 * 2**20
        ),
    )(
        diffusivity,
        salinity,
        salinity,
        salinity,
        lower,
        upper,
        south,
        north,
        west,
        east,
        rimmed,
        ty,
        tx,
        ry,
        rx,
    )


def side_layers(cells, axis, dim):
    count = lax.axis_size(axis)
    extent = cells.shape[dim]
    head = lax.slice_in_dim(cells, 0, 1, axis=dim)
    tail = lax.slice_in_dim(cells, extent - 1, extent, axis=dim)
    return (
        lax.ppermute(tail, axis, [(i, (i + 1) % count) for i in range(count)]),
        lax.ppermute(head, axis, [((i + 1) % count, i) for i in range(count)]),
    )


def scatter_columns(lines):
    count = lax.axis_size("gx")
    lead = lines.ndim - 2
    rows, length = lines.shape[-2:]
    pieces = lines.reshape(lines.shape[:-1] + (count, length // count))
    pieces = jnp.moveaxis(pieces, lead + 1, 0)
    landed = lax.all_to_all(pieces, "gx", split_axis=0, concat_axis=0, tiled=True)
    landed = jnp.moveaxis(landed, 0, lead)
    return landed.reshape(lines.shape[:-2] + (count * rows, length // count))


def per_device(coarse_modes, salinity, viscosity, forcing_gain, diffusivity):
    planes = coarse_modes.shape[2]
    row_count = coarse_modes.shape[3]
    width = coarse_modes.shape[4]
    groups = lax.axis_size("grp")
    quarter = planes // groups
    halos = (
        side_layers(salinity, "grp", 0)
        + side_layers(salinity, "gy", 1)
        + side_layers(salinity, "gx", 2)
    )
    pencil = lax.all_to_all(coarse_modes[0], "gx", split_axis=2, concat_axis=3, tiled=True)
    physical = fourier_lines(pencil[0], pencil[1], 1.0, False)
    blocks = scatter_columns(physical)
    received = lax.all_to_all(
        blocks.reshape(groups, quarter, row_count, width),
        "grp",
        split_axis=0,
        concat_axis=0,
        tiled=True,
    )
    rimmed = extended(received, (("gx", 3), ("gy", 2)), 1)
    salinity_next, restricted = fine_update(rimmed, salinity, halos, diffusivity)
    columns = lax.all_to_all(restricted, "gx", split_axis=1, concat_axis=2, tiled=True)
    spec_real, spec_imag = fourier_lines(columns, None, -1.0, True)
    own_spectra = scatter_columns(jnp.stack([spec_real, spec_imag]))
    spectrum = lax.all_to_all(
        jnp.broadcast_to(own_spectra[None], (groups,) + own_spectra.shape),
        "grp",
        split_axis=0,
        concat_axis=0,
        tiled=True,
    )
    spectrum = jnp.moveaxis(spectrum, 0, 1).reshape((2, planes) + own_spectra.shape[2:])
    total_modes = width * lax.axis_size("gx")
    mode_index = lax.axis_index("gx") * width + lax.broadcasted_iota(jnp.int32, (width,), 0)
    wavenumber = jnp.where(mode_index < total_modes // 2, mode_index, mode_index - total_modes)
    scaled_wave = 2.0 * math.pi / total_modes * wavenumber.astype(jnp.float32)
    damping = jnp.exp(-viscosity[0] * scaled_wave * scaled_wave)
    coarse_next = damping * coarse_modes + forcing_gain[0] * spectrum[None]
    return (salinity_next, coarse_next)


def solution(mesh):
    return jax.shard_map(
        per_device,
        mesh=mesh,
        in_specs=(
            P("grp", None, None, "gy", "gx"),
            P("grp", "gy", "gx"),
            P("grp"),
            P("grp"),
            P("grp"),
        ),
        out_specs=(P("grp", "gy", "gx"), P("grp", None, None, "gy", "gx")),
        check_vma=False,
    )
```
